32 devices in a mesh: row: 8 (over z, y), col: 4 (over x, core).
Axes of the slice: x: 2, y: 2, z: 4, core: 2. Of those that a mesh axis runs over, the one named last changes fastest.
Arguments:
- panel_block: float32 [16384, 128], P(('row', 'col')), may hold values from -360 to 360
- trailing: float32 [16384, 2048], P('row', 'col'), may hold values from -2048 to 2048
Outputs:
- r_scaled: float32 [128, 128], replicated
- w_scaled: float32 [128, 2048], P(None, 'col')
- remainder: float32 [16384, 2048], P('row', 'col')
The draws below stay inside these ranges and needn't reach their ends.
All inputs are finite; a program needn't handle non-finite values.
Results may differ from the reference program's by a relative error of at most 0.0003.
Values sent between devices are 32-bit elements; how exact they have to be, the bound alone decides.
No kernel may reach another device: no remote copies, remote signals or barrier semaphores. Data moves between devices by JAX's collectives and lax.ppermute only.
A program may use at most 64 MiB of HBM per device.

```python
import math
import jax
import jax.numpy as jnp
from jax import lax

NB = 128
CT = 2048
ROWS = 16384


def panel_values(key):
    key_list = jax.random.split(key, 3)
    values = jnp.clip(jax.random.normal(key_list[0], (ROWS, NB), jnp.float32), -4.0, 4.0)
    row_scale = jnp.exp(jax.random.uniform(key_list[1], (ROWS, 1), jnp.float32, 0.0, math.log(10.0)))
    rising = 1.0 + 2.0 * jnp.arange(ROWS, dtype=jnp.float32) / max(ROWS - 1, 1)
    row_scale = row_scale * rising[:, None]
    col_scale = jnp.exp(jax.random.uniform(key_list[2], (1, NB), jnp.float32, math.log(0.3), math.log(3.0)))
    return row_scale * col_scale * values


def draw_panel_block(key, part):
    return panel_values(jax.random.fold_in(key, 11))


def draw_trailing(key, part):
    base = panel_values(jax.random.fold_in(key, 11))
    mixing = jnp.clip(jax.random.normal(jax.random.fold_in(key, 23), (NB, CT), jnp.float32), -4.0, 4.0)
    mixing = mixing / (8.0 * math.sqrt(NB))
    noise_part = jnp.clip(jax.random.normal(jax.random.fold_in(key, 37), (ROWS, CT), jnp.float32), -4.0, 4.0)
    return jnp.dot(base, mixing, precision=lax.Precision.HIGHEST) + noise_part


def setup_inputs(seed: int = 0) -> dict:
    keys = jax.random.split(jax.random.key(seed), 3)
    panel_block = draw_panel_block(jax.random.fold_in(keys[2], 71), 0)
    trailing = draw_trailing(jax.random.fold_in(keys[2], 71), 0)
    return dict(panel_block=panel_block, trailing=trailing)


def reference(panel_block, trailing):
    basis, factor = jnp.linalg.qr(panel_block)
    sign_fix = jnp.sign(jnp.diagonal(factor))
    factor = factor * sign_fix[:, None]
    basis = basis * sign_fix[None, :]
    weights = jnp.dot(basis.T, trailing, precision=lax.Precision.HIGHEST)
    remainder = trailing - jnp.dot(basis, weights, precision=lax.Precision.HIGHEST)
    norm_scale = 1.0 / math.sqrt(ROWS)
    return (factor * norm_scale, weights * norm_scale, remainder)
```

```python
import functools
import math

import jax
import jax.numpy as jnp
from jax import lax
from jax.experimental import pallas as pl
from jax.experimental.pallas import tpu as pltpu
from jax.sharding import PartitionSpec as P

HIGHEST = lax.Precision.HIGHEST
VMEM = pl.BlockSpec(memory_space=pltpu.VMEM)
SMEM = pl.BlockSpec(memory_space=pltpu.SMEM)
ANY = pl.BlockSpec(memory_space=pl.ANY)


def limit(mebibytes):
    return pltpu.CompilerParams(vmem_limit_bytes=mebibytes << 20)


def f32(*shape):
    return jax.ShapeDtypeStruct(shape, jnp.float32)


def split(value):
    high = value.astype(jnp.bfloat16)
    return high, (value - high.astype(jnp.float32)).astype(jnp.bfloat16)


def dot(first, second, dims, precision=None):
    return lax.dot_general(
        first, second, (dims, ((), ())), precision=precision, preferred_element_type=jnp.float32
    )


def gram_kernel(panel_ref, gram_ref):
    panel = panel_ref[...]
    gram_ref[...] = dot(panel, panel, ((0,), (0,)), HIGHEST)


def factor_kernel(gram_ref, factor_ref, inverse_ref, *, block, step):
    width = gram_ref.shape[0]
    local = lax.broadcasted_iota(jnp.int32, (step, 1), 0)
    lanes = lax.broadcasted_iota(jnp.int32, (block, width), 1)
    rows = lax.broadcasted_iota(jnp.int32, (block, width), 0)
    factor_rows, inverse_rows = [], []
    for first in range(0, width, block):
        left = gram_ref[first : first + block, :]
        right = jnp.where(lanes == rows + first, 1.0, 0.0)
        if factor_rows:
            above = jnp.concatenate(factor_rows, 0)
            both = jnp.concatenate([above, jnp.concatenate(inverse_rows, 0)], 1)
            update = dot(above[:, first : first + block], both, ((0,), (0,)), HIGHEST)
            left = left - update[:, :width]
            right = right - update[:, width:]
        left_done, right_done = [], []
        for start in range(first, first + block, step):
            columns = [
                jnp.broadcast_to(left[:, start + j : start + j + 1], left.shape) for j in range(step)
            ]
            pivots = jnp.ones((step, width), jnp.float32)
            for k in range(step):
                pivot = columns[k][k : k + 1, :]
                pivots = jnp.where(local == k, pivot, pivots)
                ratio = columns[k] * (1.0 / pivot)
                head = jnp.where(local > k, ratio[:step], 0.0)
                if ratio.shape[0] > step:
                    head = jnp.concatenate([head, ratio[step:]], 0)
                ratio = head
                for j in range(k + 1, step):
                    columns[j] = columns[j] - ratio * columns[j][k : k + 1, :]
                left = left - ratio * left[k : k + 1, :]
                right = right - ratio * right[k : k + 1, :]
            scale = lax.rsqrt(pivots)
            left_done.append(left[:step] * scale)
            right_done.append(right[:step] * scale)
            left, right = left[step:], right[step:]
        factor_rows.append(jnp.where(lanes >= rows + first, jnp.concatenate(left_done, 0), 0.0))
        inverse_rows.append(jnp.where(lanes <= rows + first, jnp.concatenate(right_done, 0), 0.0))
        factor_ref[first : first + block, :] = factor_rows[-1]
        inverse_ref[first : first + block, :] = inverse_rows[-1]


def cross_kernel(place_ref, *refs, order):
    pieces = refs[: len(order)]
    trailing_ref, mine_ref, other_ref, split_ref, buffer, total, sems = refs[len(order) :]
    piece_rows, width = pieces[0].shape
    half = width // 2

    def rows_of(index):
        return pl.ds(pl.multiple_of((place_ref[0] ^ order[index]) * piece_rows, piece_rows), piece_rows)

    copies = [
        pltpu.make_async_copy(trailing_ref.at[rows_of(i)], buffer.at[i], sems.at[i])
        for i in range(len(order))
    ]
    for copy in copies:
        copy.start()
    for i, piece in enumerate(pieces):
        high, low = split(piece[...])
        split_ref[rows_of(i), :width] = high
        split_ref[rows_of(i), width:] = low
        copies[i].wait()
        block_high, block_low = split(buffer[i])
        contract = ((0,), (0,))
        product = dot(high, block_high, contract)
        product += dot(high, block_low, contract) + dot(low, block_high, contract)
        total[...] = product if i == 0 else total[...] + product
    bit = place_ref[1]
    mine_ref[...] = total[pl.ds(pl.multiple_of(bit * half, half), half), :]
    other_ref[...] = total[pl.ds(pl.multiple_of((1 - bit) * half, half), half), :]


def final_kernel(
    place_ref, factor_ref, inverse_ref, mine_ref, other_ref, split_ref, trailing_ref,
    r_ref, w_ref, remainder_ref, buffer, result, in_sems, out_sems, *, norm_scale,
):
    blocks, block_rows, _ = buffer.shape
    width = factor_ref.shape[0]
    reads = [
        pltpu.make_async_copy(
            trailing_ref.at[pl.ds(i * block_rows, block_rows)], buffer.at[i], in_sems.at[i]
        )
        for i in range(blocks)
    ]
    for read in reads:
        read.start()
    low_first = place_ref[1] == 0
    mine, other = mine_ref[...], other_ref[...]
    cross = jnp.concatenate(
        [jnp.where(low_first, mine, other), jnp.where(low_first, other, mine)], 0
    )
    inverse = inverse_ref[...]
    weights = dot(inverse, cross, ((1,), (0,)), HIGHEST)
    coeffs = dot(inverse, weights, ((0,), (0,)), HIGHEST)
    r_ref[...] = factor_ref[...] * norm_scale
    w_ref[...] = weights * norm_scale
    coeff_high, coeff_low = split(coeffs)
    writes = []
    for i in range(blocks):
        rows = pl.ds(i * block_rows, block_rows)
        high, low = split_ref[rows, :width], split_ref[rows, width:]
        contract = ((1,), (0,))
        product = dot(high, coeff_high, contract)
        product += dot(high, coeff_low, contract) + dot(low, coeff_high, contract)
        reads[i].wait()
        result[i] = buffer[i] - product
        write = pltpu.make_async_copy(result.at[i], remainder_ref.at[rows], out_sems.at[i])
        write.start()
        writes.append(write)
    for write in writes:
        write.wait()


def swap(value, axis, bit):
    size = lax.axis_size(axis)
    return lax.ppermute(value, axis, [(i, i ^ bit) for i in range(size)])


def bits_of(axis):
    size = lax.axis_size(axis)
    assert size & (size - 1) == 0
    return [1 << b for b in range(size.bit_length() - 1)]


def body(panel_block, trailing):
    row_bits, col_bits = bits_of("row"), bits_of("col")
    piece_rows, width = panel_block.shape
    trailing_rows, columns = trailing.shape
    half = width // 2
    total_rows = trailing_rows * lax.axis_size("row")
    norm_scale = 1.0 / math.sqrt(total_rows)
    place = jnp.stack([lax.axis_index("col"), lax.axis_index("row") & 1])

    pieces, order = [panel_block], [0]
    for bit in reversed(col_bits):
        pieces = pieces + [swap(piece, "col", bit) for piece in pieces]
        order = order + [o ^ bit for o in order]

    gram = pl.pallas_call(
        gram_kernel, out_shape=f32(width, width), in_specs=[VMEM], out_specs=VMEM,
        compiler_params=limit(4), name="gram",
    )(panel_block)
    for axis, bit in [("col", col_bits[0])] + [("row", b) for b in row_bits] + [("col", b) for b in col_bits[1:]]:
        gram = gram + swap(gram, axis, bit)
    factor, inverse = pl.pallas_call(
        functools.partial(factor_kernel, block=32, step=8),
        out_shape=(f32(width, width), f32(width, width)),
        in_specs=[VMEM], out_specs=(VMEM, VMEM), compiler_params=limit(4), name="factor",
    )(gram)

    mine, other, panel_split = pl.pallas_call(
        functools.partial(cross_kernel, order=tuple(order)),
        out_shape=(
            f32(half, columns), f32(half, columns),
            jax.ShapeDtypeStruct((trailing_rows, 2 * width), jnp.bfloat16),
        ),
        in_specs=[SMEM] + [VMEM] * len(order) + [ANY],
        out_specs=(VMEM, VMEM, VMEM),
        scratch_shapes=[
            pltpu.VMEM((len(order), piece_rows, columns), jnp.float32),
            pltpu.VMEM((width, columns), jnp.float32),
            pltpu.SemaphoreType.DMA((len(order),)),
        ],
        compiler_params=limit(20),
        name="cross",
    )(place, *pieces, trailing)
    mine = mine + swap(other, "row", row_bits[0])
    for bit in row_bits[1:]:
        mine = mine + swap(mine, "row", bit)
    other = swap(mine, "row", row_bits[0])

    blocks = 8
    return pl.pallas_call(
        functools.partial(final_kernel, norm_scale=norm_scale),
        out_shape=(f32(width, width), f32(width, columns), f32(trailing_rows, columns)),
        in_specs=[SMEM] + [VMEM] * 5 + [ANY],
        out_specs=(VMEM, VMEM, ANY),
        scratch_shapes=[
            pltpu.VMEM((blocks, trailing_rows // blocks, columns), jnp.float32),
            pltpu.VMEM((blocks, trailing_rows // blocks, columns), jnp.float32),
            pltpu.SemaphoreType.DMA((blocks,)),
            pltpu.SemaphoreType.DMA((blocks,)),
        ],
        compiler_params=limit(20),
        name="final",
    )(place, factor, inverse, mine, other, panel_split, trailing)


def solution(mesh):
    in_specs = (P(("row", "col"), None), P("row", "col"))
    out_specs = (P(), P(None, "col"), P("row", "col"))
    return jax.shard_map(body, mesh=mesh, in_specs=in_specs, out_specs=out_specs, check_vma=False)
```

```python
import functools
import math

import jax
import jax.numpy as jnp
from jax import lax
from jax.experimental import pallas as pl
from jax.experimental.pallas import tpu as pltpu
from jax.sharding import PartitionSpec as P


HIGHEST = lax.Precision.HIGHEST
ROOM = 48
CUTS = 4
VMEM = pl.BlockSpec(memory_space=pltpu.VMEM)
HBM = pl.BlockSpec(memory_space=pltpu.HBM)


def limit(mebibytes):
    return pltpu.CompilerParams(vmem_limit_bytes=mebibytes << 20)


def f32(*shape):
    return jax.ShapeDtypeStruct(shape, jnp.float32)


def split(value):
    high = value.astype(jnp.bfloat16)
    return high, (value - high.astype(jnp.float32)).astype(jnp.bfloat16)


def store_split(split_ref, piece):
    width = piece.shape[1]
    split_ref[:, :width], split_ref[:, width:] = split(piece)


def cross_of(split_ref, block):
    width = split_ref.shape[1] // 2
    high, low = split_ref[:, :width], split_ref[:, width:]
    block_high, block_low = split(block)
    contract = ((0,), (0,))
    product = dot(high, block_high, contract)
    return product + dot(high, block_low, contract) + dot(low, block_high, contract)


def dot(first, second, dims, precision=None):
    return lax.dot_general(
        first, second, (dims, ((), ())), precision=precision, preferred_element_type=jnp.float32
    )


def block_of(offset, rows):
    return (lax.axis_index("col") ^ offset) * rows


def copy_in(source, first, target, sems):
    rows = target.shape[0] // CUTS
    copies = []
    for k in range(CUTS):
        where = pl.ds(pl.multiple_of(first + k * rows, rows), rows)
        copies.append(pltpu.make_async_copy(source.at[where], target.at[pl.ds(k * rows, rows)], sems.at[k]))
        copies[-1].start()
    return copies


def part_of(offset, group):
    return (lax.axis_index("row") & (group - 1)) ^ offset


def wait_all(copies):
    for copy in copies:
        copy.wait()


def own_kernel(panel_ref, gram_ref, split_ref):
    panel = panel_ref[...]
    gram_ref[...] = dot(panel, panel, ((0,), (0,)), HIGHEST)
    store_split(split_ref, panel)


def mate_kernel(mate_ref, gram_in_ref, gram_ref, split_ref, sum_ref, *, near):
    mate = mate_ref[...]
    half = mate.shape[1] // 2
    sum_ref[...] = gram_in_ref[...] + dot(mate, mate, ((0,), (0,)), HIGHEST)
    upper = jnp.where((lax.axis_index("col") & near) == 0, 0, half)
    gram_ref[...] = sum_ref[pl.ds(pl.multiple_of(upper, half), half), :]
    store_split(split_ref, mate)


def near_kernel(own_ref, mate_ref, trailing_ref, cross_ref, *refs, order):
    held_refs, sems = refs[: len(order)], refs[len(order)]
    rows = own_ref.shape[0]
    copies = [
        copy_in(trailing_ref, block_of(offset, rows), held_ref, sems.at[i])
        for i, (offset, held_ref) in enumerate(zip(order, held_refs))
    ]
    wait_all(copies[0])
    total = cross_of(own_ref, held_refs[0][...])
    wait_all(copies[1])
    cross_ref[...] = total + cross_of(mate_ref, held_refs[1][...])
    for rest in copies[2:]:
        wait_all(rest)


def far_kernel(piece_ref, held_ref, cross_in_ref, split_ref, cross_ref):
    store_split(split_ref, piece_ref[...])
    cross_ref[...] = cross_in_ref[...] + cross_of(split_ref, held_ref[...])


def last_kernel(piece_ref, held_ref, cross_in_ref, split_ref, *refs):
    *part_refs, sum_ref = refs
    store_split(split_ref, piece_ref[...])
    sum_ref[...] = cross_in_ref[...] + cross_of(split_ref, held_ref[...])
    part = part_refs[0].shape[1]
    for k, part_ref in enumerate(part_refs):
        first = pl.multiple_of(part_of(k, len(part_refs)) * part, part)
        part_ref[...] = sum_ref[:, pl.ds(first, part)]


def factor_kernel(mine_ref, other_ref, scaled_ref, solve_ref, *, near, block, step, norm_scale):
    width = mine_ref.shape[1]
    first_half = (lax.axis_index("col") & near) == 0
    mine, other = mine_ref[...], other_ref[...]
    gram = jnp.concatenate(
        [jnp.where(first_half, mine, other), jnp.where(first_half, other, mine)], 0
    )
    local = lax.broadcasted_iota(jnp.int32, (step, 1), 0)
    lanes = lax.broadcasted_iota(jnp.int32, (block, width), 1)
    rows = lax.broadcasted_iota(jnp.int32, (block, width), 0)
    factor_rows, inverse_rows = [], []
    for first in range(0, width, block):
        left = gram[first : first + block, :]
        right = jnp.where(lanes == rows + first, 1.0, 0.0)
        if factor_rows:
            above = jnp.concatenate(factor_rows, 0)
            both = jnp.concatenate([above, jnp.concatenate(inverse_rows, 0)], 1)
            update = dot(above[:, first : first + block], both, ((0,), (0,)), HIGHEST)
            left = left - update[:, :width]
            right = right - update[:, width:]
        left_done, right_done = [], []
        for start in range(first, first + block, step):
            columns = [
                jnp.broadcast_to(left[:, start + j : start + j + 1], left.shape) for j in range(step)
            ]
            pivots = jnp.ones((step, width), jnp.float32)
            for k in range(step):
                pivot = columns[k][k : k + 1, :]
                pivots = jnp.where(local == k, pivot, pivots)
                ratio = columns[k] * (1.0 / pivot)
                head = jnp.where(local > k, ratio[:step], 0.0)
                if ratio.shape[0] > step:
                    head = jnp.concatenate([head, ratio[step:]], 0)
                ratio = head
                for j in range(k + 1, step):
                    columns[j] = columns[j] - ratio * columns[j][k : k + 1, :]
                left = left - ratio * left[k : k + 1, :]
                right = right - ratio * right[k : k + 1, :]
            scale = lax.rsqrt(pivots)
            left_done.append(left[:step] * scale)
            right_done.append(right[:step] * scale)
            left, right = left[step:], right[step:]
        factor_rows.append(jnp.where(lanes >= rows + first, jnp.concatenate(left_done, 0), 0.0))
        inverse_rows.append(jnp.where(lanes <= rows + first, jnp.concatenate(right_done, 0), 0.0))
        scaled_ref[first : first + block, :] = factor_rows[-1] * norm_scale
    inverse = jnp.concatenate(inverse_rows, 0)
    solve = jnp.concatenate([inverse, dot(inverse, inverse, ((0,), (0,)), HIGHEST)], 0)
    store_split(solve_ref, solve)


def basis_kernel(solve_ref, *refs):
    *split_refs, out_ref = refs
    width = solve_ref.shape[1] // 2
    high, low = solve_ref[width:, :width], solve_ref[width:, width:]
    right = jnp.concatenate([high, high, low], 0)
    rows = split_refs[0].shape[0]
    for i, split_ref in enumerate(split_refs):
        both = split_ref[...]
        left = jnp.concatenate([both, both[:, :width]], 1)
        store_split(out_ref.at[i * rows : (i + 1) * rows], dot(left, right, ((1,), (0,))))


def final_kernel(solve_ref, basis_ref, *refs, order, parts, group, norm_scale, chunk, last):
    held_refs, refs = refs[: len(order)], refs[len(order) :]
    cross_refs, refs = refs[: len(parts)], refs[len(parts) :]
    if last:
        w_before_ref, _, w_ref, remainder_ref, result, sems = refs
    else:
        w_ref, remainder_ref, result, sems = refs
    width, part = cross_refs[0].shape
    cross = jnp.concatenate([ref[...] for ref in cross_refs], 1)
    high, low = split(cross)
    right = jnp.concatenate([high, high, low], 0)
    contract = ((1,), (0,))
    columns = [pl.ds(pl.multiple_of(part_of(k, group) * part, part), part) for k in parts]
    writes = []
    for i, held_ref in enumerate(held_refs):
        rows = held_ref.shape[0]
        where = pl.ds(pl.multiple_of(block_of(order[i], rows), rows), rows)
        for first in range(0, rows, chunk):
            here = slice(first, first + chunk)
            both = basis_ref[i * rows + first : i * rows + first + chunk, :]
            product = dot(jnp.concatenate([both, both[:, :width]], 1), right, contract)
            for j, column in enumerate(columns):
                result[i, j, here, :] = held_ref[here, column] - product[:, j * part : (j + 1) * part]
        for j, column in enumerate(columns):
            write = pltpu.make_async_copy(
                result.at[i, j], remainder_ref.at[where, column], sems.at[i, j]
            )
            write.start()
            writes.append(write)
    inverse = solve_ref[:width, :]
    weights = dot(jnp.concatenate([inverse, inverse[:, :width]], 1), right, contract) * norm_scale
    if last:
        w_ref[...] = w_before_ref[...]
    for j, column in enumerate(columns):
        w_ref[:, column] = weights[:, j * part : (j + 1) * part]
    wait_all(writes)


def swap(value, axis, bit):
    size = lax.axis_size(axis)
    return lax.ppermute(value, axis, [(i, i ^ bit) for i in range(size)])


def bits_of(axis):
    size = lax.axis_size(axis)
    assert size & (size - 1) == 0
    return [1 << b for b in range(size.bit_length() - 1)]


def body(panel_block, trailing):
    row_bits, col_bits = bits_of("row"), bits_of("col")
    near, far_bits = col_bits[0], col_bits[1:]
    piece_rows, width = panel_block.shape
    trailing_rows, columns = trailing.shape
    group_bits = row_bits[:2]
    group = 1 << len(group_bits)
    part = columns // group
    total_rows = trailing_rows * lax.axis_size("row")
    norm_scale = 1.0 / math.sqrt(total_rows)

    far, offsets = [panel_block], [0]
    for bit in far_bits:
        far = far + [swap(piece, "col", bit) for piece in far]
        offsets = offsets + [o ^ bit for o in offsets]
    mate = swap(panel_block, "col", near)
    last = [swap(piece, "col", near) for piece in far[1:]]
    order = [0, near] + offsets[1:] + [o ^ near for o in offsets[1:]]

    square, wide = f32(width, width), f32(width, columns)
    half_square, block = f32(width // 2, width), f32(piece_rows, columns)
    split_shape = jax.ShapeDtypeStruct((piece_rows, 2 * width), jnp.bfloat16)
    copies = pltpu.SemaphoreType.DMA
    gram, own_split = pl.pallas_call(
        own_kernel, out_shape=(square, split_shape), in_specs=[VMEM], out_specs=(VMEM,) * 2,
        compiler_params=limit(8), name="own",
    )(panel_block)
    gram, mate_split = pl.pallas_call(
        functools.partial(mate_kernel, near=near),
        out_shape=(half_square, split_shape), in_specs=[VMEM] * 2, out_specs=(VMEM,) * 2,
        scratch_shapes=[pltpu.VMEM((width, width), jnp.float32)],
        compiler_params=limit(8), name="mate",
    )(mate, gram)
    cross, *held = pl.pallas_call(
        functools.partial(near_kernel, order=order),
        out_shape=(wide,) + (block,) * len(order),
        in_specs=[VMEM, VMEM, HBM], out_specs=(VMEM,) * (1 + len(order)),
        scratch_shapes=[copies((len(order), CUTS))], compiler_params=limit(ROOM), name="near",
    )(own_split, mate_split, trailing)
    splits = [own_split, mate_split]
    pieces = far[1:] + last
    for i, piece in enumerate(pieces[:-1]):
        split_out, cross = pl.pallas_call(
            far_kernel, out_shape=(split_shape, wide), in_specs=[VMEM] * 3,
            out_specs=(VMEM,) * 2, compiler_params=limit(16), name="far",
        )(piece, held[i + 2], cross)
        splits.append(split_out)
    split_out, *parts = pl.pallas_call(
        last_kernel,
        out_shape=(split_shape,) + (f32(width, part),) * group,
        in_specs=[VMEM] * 3, out_specs=(VMEM,) * (1 + group),
        scratch_shapes=[pltpu.VMEM((width, columns), jnp.float32)],
        compiler_params=limit(16), name="last",
    )(pieces[-1], held[-1], cross)
    splits.append(split_out)

    gram = gram + sum(swap(gram, "row", k) for k in range(1, group))
    for axis, bit in [("row", b) for b in row_bits[len(group_bits) :]] + [("col", b) for b in far_bits]:
        gram = gram + swap(gram, axis, bit)
    other_half = swap(gram, "col", near)
    r_scaled, solve = pl.pallas_call(
        functools.partial(factor_kernel, near=near, block=32, step=8, norm_scale=norm_scale),
        out_shape=(square, jax.ShapeDtypeStruct((2 * width, 2 * width), jnp.bfloat16)),
        in_specs=[VMEM, VMEM], out_specs=(VMEM, VMEM), compiler_params=limit(4), name="factor",
    )(gram, other_half)
    mine = parts[0]
    for k in range(1, group):
        mine = mine + swap(parts[k], "row", k)
    for bit in row_bits[len(group_bits) :]:
        mine = mine + swap(mine, "row", bit)
    others = [swap(mine, "row", k) for k in range(1, group)]

    basis = pl.pallas_call(
        basis_kernel,
        out_shape=jax.ShapeDtypeStruct((trailing_rows, 2 * width), jnp.bfloat16),
        in_specs=[VMEM] * (1 + len(splits)), out_specs=VMEM, compiler_params=limit(8), name="basis",
    )(solve, *splits)
    def final(ks, *before):
        given = [mine, *others]
        operands = (solve, basis, *held, *[given[k] for k in ks])
        return pl.pallas_call(
            functools.partial(
                final_kernel, order=order, parts=ks, group=group, norm_scale=norm_scale,
                chunk=128, last=bool(before),
            ),
            out_shape=(wide, f32(trailing_rows, columns)),
            in_specs=[VMEM] * len(operands) + [VMEM, HBM][: len(before)], out_specs=(VMEM, HBM),
            scratch_shapes=[
                pltpu.VMEM((len(order), len(ks), piece_rows, part), jnp.float32),
                copies((len(order), len(ks))),
            ],
            input_output_aliases={len(operands) + 1: 1} if before else {},
            compiler_params=limit(20),
        )(*operands, *before)

    first = (0, group - 1)
    before = final(first)
    rest = tuple(k for k in range(group) if k not in first)
    w_scaled, remainder = final(rest, *before) if rest else before
    return r_scaled, w_scaled, remainder


def solution(mesh):
    in_specs = (P(("row", "col"), None), P("row", "col"))
    out_specs = (P(), P(None, "col"), P("row", "col"))

    return jax.shard_map(body, mesh=mesh, in_specs=in_specs, out_specs=out_specs, check_vma=False)
```

```python
import functools
import math

import jax
import jax.numpy as jnp
from jax import lax
from jax.experimental import pallas as pl
from jax.experimental.pallas import tpu as pltpu
from jax.sharding import PartitionSpec as P


HIGHEST = lax.Precision.HIGHEST
CUTS = 2
BLOCK, STEP = 32, 16
COST = pl.CostEstimate(flops=1 << 31, bytes_accessed=1 << 23, transcendentals=0)
CHUNK = 128
VMEM = pl.BlockSpec(memory_space=pltpu.VMEM)
HBM = pl.BlockSpec(memory_space=pltpu.HBM)


def limit(mebibytes):
    return pltpu.CompilerParams(vmem_limit_bytes=mebibytes << 20)


def f32(*shape):
    return jax.ShapeDtypeStruct(shape, jnp.float32)


def split(value):
    high = value.astype(jnp.bfloat16)
    return high, (value - high.astype(jnp.float32)).astype(jnp.bfloat16)


def store_split(split_ref, piece):
    width = piece.shape[1]
    split_ref[:, :width], split_ref[:, width:] = split(piece)


def cross_of(split_ref, block):
    width = split_ref.shape[1] // 2
    high, low = split_ref[:, :width], split_ref[:, width:]
    block_high, block_low = split(block)
    contract = ((0,), (0,))
    product = dot(high, block_high, contract)
    return product + dot(high, block_low, contract) + dot(low, block_high, contract)


def dot(first, second, dims, precision=None):
    return lax.dot_general(
        first, second, (dims, ((), ())), precision=precision, preferred_element_type=jnp.float32
    )


def block_of(offset, rows):
    return (lax.axis_index("col") ^ offset) * rows


def part_of(offset, group):
    return (lax.axis_index("row") & (group - 1)) ^ offset


def wait_all(copies):
    for copy in copies:
        copy.wait()


def own_kernel(panel_ref, gram_ref, split_ref):
    panel = panel_ref[...]
    gram_ref[...] = dot(panel, panel, ((0,), (0,)), HIGHEST)
    store_split(split_ref, panel)


def mate_kernel(mate_ref, gram_in_ref, gram_ref, split_ref, sum_ref, *, near):
    mate = mate_ref[...]
    half = mate.shape[1] // 2
    sum_ref[...] = gram_in_ref[...] + dot(mate, mate, ((0,), (0,)), HIGHEST)
    upper = jnp.where((lax.axis_index("col") & near) == 0, 0, half)
    gram_ref[...] = sum_ref[pl.ds(pl.multiple_of(upper, half), half), :]
    store_split(split_ref, mate)


def rows_of(held_ref, offset, rows):
    return held_ref[pl.ds(pl.multiple_of(block_of(offset, rows), rows), rows), :]


def near_kernel(own_ref, mate_ref, held_ref, cross_ref, *, order):
    rows = own_ref.shape[0]
    total = cross_of(own_ref, rows_of(held_ref, order[0], rows))
    cross_ref[...] = total + cross_of(mate_ref, rows_of(held_ref, order[1], rows))


def far_kernel(piece_ref, held_ref, cross_in_ref, split_ref, cross_ref, *, offset):
    store_split(split_ref, piece_ref[...])
    block = rows_of(held_ref, offset, piece_ref.shape[0])
    cross_ref[...] = cross_in_ref[...] + cross_of(split_ref, block)


def last_kernel(piece_ref, held_ref, cross_in_ref, split_ref, *refs, offset):
    *part_refs, sum_ref = refs
    store_split(split_ref, piece_ref[...])
    block = rows_of(held_ref, offset, piece_ref.shape[0])
    sum_ref[...] = cross_in_ref[...] + cross_of(split_ref, block)
    part = part_refs[0].shape[1]
    for k, part_ref in enumerate(part_refs):
        first = pl.multiple_of(part_of(k, len(part_refs)) * part, part)
        part_ref[...] = sum_ref[:, pl.ds(first, part)]


def factor_kernel(*refs, near, block, step, norm_scale):
    *half_refs, scaled_ref, solve_ref = refs
    width = scaled_ref.shape[1]
    first_half = (lax.axis_index("col") & near) == 0
    mine, other = (sum(ref[...] for ref in half_refs[k::2]) for k in range(2))
    gram = jnp.concatenate(
        [jnp.where(first_half, mine, other), jnp.where(first_half, other, mine)], 0
    )
    local = lax.broadcasted_iota(jnp.int32, (step, 1), 0)
    lanes = lax.broadcasted_iota(jnp.int32, (block, width), 1)
    rows = lax.broadcasted_iota(jnp.int32, (block, width), 0)
    factor_rows, inverse_rows = [], []
    for first in range(0, width, block):
        left = gram[first : first + block, :]
        right = jnp.where(lanes == rows + first, 1.0, 0.0)
        if factor_rows:
            above = jnp.concatenate(factor_rows, 0)
            both = jnp.concatenate([above, jnp.concatenate(inverse_rows, 0)], 1)
            update = dot(above[:, first : first + block], both, ((0,), (0,)), HIGHEST)
            left = left - update[:, :width]
            right = right - update[:, width:]
        left_done, right_done = [], []
        for start in range(first, first + block, step):
            columns = [
                jnp.broadcast_to(left[:, start + j : start + j + 1], left.shape) for j in range(step)
            ]
            pivots = jnp.ones((step, width), jnp.float32)
            for k in range(step):
                pivot = columns[k][k : k + 1, :]
                pivots = jnp.where(local == k, pivot, pivots)
                ratio = columns[k] * (1.0 / pivot)
                for j in range(k + 1, step):
                    columns[j] = columns[j] - ratio * columns[j][k : k + 1, :]
                head = jnp.where(local > k, ratio[:step], 0.0)
                if ratio.shape[0] > step:
                    head = jnp.concatenate([head, ratio[step:]], 0)
                ratio = head
                left = left - ratio * left[k : k + 1, :]
                right = right - ratio * right[k : k + 1, :]
            scale = lax.rsqrt(pivots)
            left_done.append(left[:step] * scale)
            right_done.append(right[:step] * scale)
            left, right = left[step:], right[step:]
        factor_rows.append(jnp.where(lanes >= rows + first, jnp.concatenate(left_done, 0), 0.0))
        inverse_rows.append(jnp.where(lanes <= rows + first, jnp.concatenate(right_done, 0), 0.0))
        scaled_ref[first : first + block, :] = factor_rows[-1] * norm_scale
    inverse = jnp.concatenate(inverse_rows, 0)
    solve = jnp.concatenate([inverse, dot(inverse, inverse, ((0,), (0,)), HIGHEST)], 0)
    store_split(solve_ref, solve)


def final_kernel(solve_ref, held_ref, *refs, order, group, norm_scale, chunk):
    split_refs, refs = refs[: len(order)], refs[len(order) :]
    part_refs, (w_ref, remainder_ref, cross_ref, w_here, result, w_sem, sems) = refs[:group], refs[group:]
    width, part = part_refs[0].shape
    for k, part_ref in enumerate(part_refs):
        cross_ref[:, pl.ds(pl.multiple_of(part_of(k, group) * part, part), part)] = part_ref[...]
    contract = ((1,), (0,))
    high, low = split(cross_ref[...])
    both = solve_ref[...]
    solved = dot(
        jnp.concatenate([both, both[:, :width]], 1), jnp.concatenate([high, high, low], 0), contract
    )
    w_here[...] = solved[:width] * norm_scale
    w_copy = pltpu.make_async_copy(w_here, w_ref, w_sem)
    w_copy.start()
    high, low = split(solved[width:])
    right = jnp.concatenate([high, high, low], 0)
    copies = [w_copy]
    rows = split_refs[0].shape[0]
    cuts = sems.shape[1]
    for i, split_ref in enumerate(split_refs):
        base = pl.multiple_of(block_of(order[i], rows), rows)
        for first in range(0, rows, chunk):
            both = split_ref[first : first + chunk, :]
            product = dot(jnp.concatenate([both, both[:, :width]], 1), right, contract)
            held = held_ref[pl.ds(pl.multiple_of(base + first, chunk), chunk), :]
            result[i, first : first + chunk, :] = held - product
            done = first + chunk
            if done % (rows // cuts) == 0:
                n = done * cuts // rows - 1
                here = pl.ds(n * (rows // cuts), rows // cuts)
                there = pl.ds(pl.multiple_of(base + n * (rows // cuts), rows // cuts), rows // cuts)
                copies.append(
                    pltpu.make_async_copy(result.at[i, here], remainder_ref.at[there], sems.at[i, n])
                )
                copies[-1].start()
    wait_all(copies)


def swap(value, axis, bit):
    size = lax.axis_size(axis)
    return lax.ppermute(value, axis, [(i, i ^ bit) for i in range(size)])


def bits_of(axis):
    size = lax.axis_size(axis)
    assert size & (size - 1) == 0
    return [1 << b for b in range(size.bit_length() - 1)]


def body(panel_block, trailing):
    row_bits, col_bits = bits_of("row"), bits_of("col")
    near, far_bits = col_bits[0], col_bits[1:]
    piece_rows, width = panel_block.shape
    trailing_rows, columns = trailing.shape
    group_bits = row_bits[:2]
    group = 1 << len(group_bits)
    part = columns // group
    total_rows = trailing_rows * lax.axis_size("row")
    norm_scale = 1.0 / math.sqrt(total_rows)

    far, offsets = [panel_block], [0]
    for bit in far_bits:
        far = far + [swap(piece, "col", bit) for piece in far]
        offsets = offsets + [o ^ bit for o in offsets]
    mate = swap(panel_block, "col", near)
    last = [swap(piece, "col", near) for piece in far[1:]]
    order = [0, near] + offsets[1:] + [o ^ near for o in offsets[1:]]

    square, wide = f32(width, width), f32(width, columns)
    half_square = f32(width // 2, width)
    split_shape = jax.ShapeDtypeStruct((piece_rows, 2 * width), jnp.bfloat16)
    copies = pltpu.SemaphoreType.DMA
    gram, own_split = pl.pallas_call(
        own_kernel, out_shape=(square, split_shape), in_specs=[VMEM], out_specs=(VMEM,) * 2,
        compiler_params=limit(8), name="own", cost_estimate=COST,
    )(pltpu.with_memory_space_constraint(panel_block, pltpu.HBM))
    gram, mate_split = pl.pallas_call(
        functools.partial(mate_kernel, near=near),
        out_shape=(half_square, split_shape), in_specs=[VMEM] * 2, out_specs=(VMEM,) * 2,
        scratch_shapes=[pltpu.VMEM((width, width), jnp.float32)],
        compiler_params=limit(8), name="mate", cost_estimate=COST,
    )(mate, gram)
    held = pltpu.with_memory_space_constraint(trailing, pltpu.VMEM)
    cross = pl.pallas_call(
        functools.partial(near_kernel, order=order), out_shape=wide,
        in_specs=[VMEM] * 3, out_specs=VMEM, compiler_params=limit(16), name="near",
    )(own_split, mate_split, held)
    splits = [own_split, mate_split]
    pieces = far[1:] + last
    for i, piece in enumerate(pieces[:-1]):
        split_out, cross = pl.pallas_call(
            functools.partial(far_kernel, offset=order[i + 2]),
            out_shape=(split_shape, wide), in_specs=[VMEM] * 3,
            out_specs=(VMEM,) * 2, compiler_params=limit(16), name="far",
        )(piece, held, cross)
        splits.append(split_out)
    split_out, *parts = pl.pallas_call(
        functools.partial(last_kernel, offset=order[-1]),
        out_shape=(split_shape,) + (f32(width, part),) * group,
        in_specs=[VMEM] * 3, out_specs=(VMEM,) * (1 + group),
        scratch_shapes=[pltpu.VMEM((width, columns), jnp.float32)],
        compiler_params=limit(16), name="last",
    )(pieces[-1], held, cross)
    splits.append(split_out)

    gram = gram + sum(swap(gram, "row", k) for k in range(1, group))
    for bit in row_bits[len(group_bits) :]:
        gram = gram + swap(gram, "row", bit)
    halves = [gram if o == 0 else swap(gram, "col", o) for f in offsets for o in (f, f ^ near)]
    r_scaled, solve = pl.pallas_call(
        functools.partial(factor_kernel, near=near, block=BLOCK, step=STEP, norm_scale=norm_scale),
        out_shape=(square, jax.ShapeDtypeStruct((2 * width, 2 * width), jnp.bfloat16)),
        in_specs=[VMEM] * len(halves), out_specs=(VMEM, VMEM), compiler_params=limit(4), name="factor",
    )(*halves)
    mine = parts[0]
    for k in range(1, group):
        mine = mine + swap(parts[k], "row", k)
    for bit in row_bits[len(group_bits) :]:
        mine = mine + swap(mine, "row", bit)
    others = [swap(mine, "row", k) for k in range(1, group)]

    w_scaled, remainder = pl.pallas_call(
        functools.partial(final_kernel, order=order, group=group, norm_scale=norm_scale, chunk=CHUNK),
        out_shape=(wide, f32(trailing_rows, columns)),
        in_specs=[VMEM] * (2 + len(order) + group), out_specs=(HBM, HBM),
        scratch_shapes=[
            pltpu.VMEM((width, columns), jnp.float32),
            pltpu.VMEM((width, columns), jnp.float32),
            pltpu.VMEM((len(order), piece_rows, columns), jnp.float32),
            copies,
            copies((len(order), CUTS)),
        ],
        compiler_params=limit(20), name="final",
    )(solve, held, *splits, mine, *others)
    return r_scaled, w_scaled, remainder


def solution(mesh):
    in_specs = (P(("row", "col"), None), P("row", "col"))
    out_specs = (P(), P(None, "col"), P("row", "col"))

    return jax.shard_map(body, mesh=mesh, in_specs=in_specs, out_specs=out_specs, check_vma=False)
```

```python
import functools
import math

import jax
import jax.numpy as jnp
from jax import lax
from jax.experimental import pallas as pl
from jax.experimental.pallas import tpu as pltpu
from jax.sharding import PartitionSpec as P


HIGHEST = lax.Precision.HIGHEST
CUTS = 2
BLOCK, STEP = 32, 16
COST = pl.CostEstimate(flops=1 << 31, bytes_accessed=1 << 23, transcendentals=0)
CHUNK = 128
VMEM = pl.BlockSpec(memory_space=pltpu.VMEM)
HBM = pl.BlockSpec(memory_space=pltpu.HBM)


def limit(mebibytes):
    return pltpu.CompilerParams(vmem_limit_bytes=mebibytes << 20)


def f32(*shape):
    return jax.ShapeDtypeStruct(shape, jnp.float32)


def split(value):
    high = value.astype(jnp.bfloat16)
    return high, (value - high.astype(jnp.float32)).astype(jnp.bfloat16)


def store_split(split_ref, piece):
    width = piece.shape[1]
    split_ref[:, :width], split_ref[:, width:] = split(piece)


def cross_of(split_ref, block):
    width = split_ref.shape[1] // 2
    high, low = split_ref[:, :width], split_ref[:, width:]
    block_high, block_low = split(block)
    contract = ((0,), (0,))
    product = dot(high, block_high, contract)
    return product + dot(high, block_low, contract) + dot(low, block_high, contract)


def dot(first, second, dims, precision=None):
    return lax.dot_general(
        first, second, (dims, ((), ())), precision=precision, preferred_element_type=jnp.float32
    )


def block_of(offset, rows):
    return (lax.axis_index("col") ^ offset) * rows


def part_of(slot, group):
    return (lax.axis_index("row") & (group - 1)) ^ slot


def wait_all(copies):
    for copy in copies:
        copy.wait()


def own_kernel(panel_ref, gram_ref, split_ref):
    panel = panel_ref[...]
    gram_ref[...] = dot(panel, panel, ((0,), (0,)), HIGHEST)
    store_split(split_ref, panel)


def mate_kernel(mate_ref, gram_in_ref, gram_ref, split_ref, sum_ref, *, near):
    mate = mate_ref[...]
    half = mate.shape[1] // 2
    sum_ref[...] = gram_in_ref[...] + dot(mate, mate, ((0,), (0,)), HIGHEST)
    upper = jnp.where((lax.axis_index("col") & near) == 0, 0, half)
    gram_ref[...] = sum_ref[pl.ds(pl.multiple_of(upper, half), half), :]
    store_split(split_ref, mate)


def rows_of(held_ref, offset, rows):
    return held_ref[pl.ds(pl.multiple_of(block_of(offset, rows), rows), rows), :]


def near_kernel(own_ref, mate_ref, held_ref, cross_ref, *, order):
    rows = own_ref.shape[0]
    total = cross_of(own_ref, rows_of(held_ref, order[0], rows))
    cross_ref[...] = total + cross_of(mate_ref, rows_of(held_ref, order[1], rows))


def far_kernel(piece_ref, held_ref, cross_in_ref, split_ref, cross_ref, *, offset):
    store_split(split_ref, piece_ref[...])
    block = rows_of(held_ref, offset, piece_ref.shape[0])
    cross_ref[...] = cross_in_ref[...] + cross_of(split_ref, block)


def last_kernel(piece_ref, held_ref, cross_in_ref, split_ref, *refs, offset):
    *part_refs, sum_ref = refs
    store_split(split_ref, piece_ref[...])
    block = rows_of(held_ref, offset, piece_ref.shape[0])
    sum_ref[...] = cross_in_ref[...] + cross_of(split_ref, block)
    part = part_refs[0].shape[1]
    for k, part_ref in enumerate(part_refs):
        first = pl.multiple_of(part_of(k, len(part_refs)) * part, part)
        part_ref[...] = sum_ref[:, pl.ds(first, part)]


def factor_kernel(*refs, near, block, step, norm_scale):
    *half_refs, scaled_ref, solve_ref = refs
    width = scaled_ref.shape[1]
    first_half = (lax.axis_index("col") & near) == 0
    mine, other = (sum(ref[...] for ref in half_refs[k::2]) for k in range(2))
    gram = jnp.concatenate(
        [jnp.where(first_half, mine, other), jnp.where(first_half, other, mine)], 0
    )
    local = lax.broadcasted_iota(jnp.int32, (step, 1), 0)
    lanes = lax.broadcasted_iota(jnp.int32, (block, width), 1)
    rows = lax.broadcasted_iota(jnp.int32, (block, width), 0)
    factor_rows, inverse_rows = [], []
    for first in range(0, width, block):
        left = gram[first : first + block, :]
        right = jnp.where(lanes == rows + first, 1.0, 0.0)
        if factor_rows:
            above = jnp.concatenate(factor_rows, 0)
            both = jnp.concatenate([above, jnp.concatenate(inverse_rows, 0)], 1)
            update = dot(above[:, first : first + block], both, ((0,), (0,)), HIGHEST)
            left = left - update[:, :width]
            right = right - update[:, width:]
        left_done, right_done = [], []
        for start in range(first, first + block, step):
            columns = [
                jnp.broadcast_to(left[:, start + j : start + j + 1], left.shape) for j in range(step)
            ]
            pivots = jnp.ones((step, width), jnp.float32)
            for k in range(step):
                pivot = columns[k][k : k + 1, :]
                pivots = jnp.where(local == k, pivot, pivots)
                ratio = columns[k] * (1.0 / pivot)
                for j in range(k + 1, step):
                    columns[j] = columns[j] - ratio * columns[j][k : k + 1, :]
                head = jnp.where(local > k, ratio[:step], 0.0)
                if ratio.shape[0] > step:
                    head = jnp.concatenate([head, ratio[step:]], 0)
                ratio = head
                left = left - ratio * left[k : k + 1, :]
                right = right - ratio * right[k : k + 1, :]
            scale = lax.rsqrt(pivots)
            left_done.append(left[:step] * scale)
            right_done.append(right[:step] * scale)
            left, right = left[step:], right[step:]
        factor_rows.append(jnp.where(lanes >= rows + first, jnp.concatenate(left_done, 0), 0.0))
        inverse_rows.append(jnp.where(lanes <= rows + first, jnp.concatenate(right_done, 0), 0.0))
        scaled_ref[first : first + block, :] = factor_rows[-1] * norm_scale
    inverse = jnp.concatenate(inverse_rows, 0)
    solve = jnp.concatenate([inverse, dot(inverse, inverse, ((0,), (0,)), HIGHEST)], 0)
    store_split(solve_ref, solve)


def final_kernel(solve_ref, held_ref, *refs, order, group, norm_scale, chunk):
    split_refs, refs = refs[: len(order)], refs[len(order) :]
    part_refs, (w_ref, remainder_ref, cross_ref, w_here, result, w_sem, sems) = refs[:group], refs[group:]
    width, part = part_refs[0].shape
    for k, part_ref in enumerate(part_refs):
        cross_ref[:, pl.ds(pl.multiple_of(part_of(k, group) * part, part), part)] = part_ref[...]
    contract = ((1,), (0,))
    high, low = split(cross_ref[...])
    both = solve_ref[...]
    solved = dot(
        jnp.concatenate([both, both[:, :width]], 1), jnp.concatenate([high, high, low], 0), contract
    )
    w_here[...] = solved[:width] * norm_scale
    w_copy = pltpu.make_async_copy(w_here, w_ref, w_sem)
    w_copy.start()
    high, low = split(solved[width:])
    right = jnp.concatenate([high, high, low], 0)
    copies = [w_copy]
    rows = split_refs[0].shape[0]
    cuts = sems.shape[1]
    for i, split_ref in enumerate(split_refs):
        base = pl.multiple_of(block_of(order[i], rows), rows)
        for first in range(0, rows, chunk):
            both = split_ref[first : first + chunk, :]
            product = dot(jnp.concatenate([both, both[:, :width]], 1), right, contract)
            held = held_ref[pl.ds(pl.multiple_of(base + first, chunk), chunk), :]
            result[i, first : first + chunk, :] = held - product
            done = first + chunk
            if done % (rows // cuts) == 0:
                n = done * cuts // rows - 1
                here = pl.ds(n * (rows // cuts), rows // cuts)
                there = pl.ds(pl.multiple_of(base + n * (rows // cuts), rows // cuts), rows // cuts)
                copies.append(
                    pltpu.make_async_copy(result.at[i, here], remainder_ref.at[there], sems.at[i, n])
                )
                copies[-1].start()
    wait_all(copies)


def swap(value, axis, bit):
    size = lax.axis_size(axis)
    return lax.ppermute(value, axis, [(i, i ^ bit) for i in range(size)])


def bits_of(axis):
    size = lax.axis_size(axis)
    assert size & (size - 1) == 0
    return [1 << b for b in range(size.bit_length() - 1)]


def body(panel_block, trailing):
    row_bits, col_bits = bits_of("row"), bits_of("col")
    near, far_bits = col_bits[0], col_bits[1:]
    piece_rows, width = panel_block.shape
    trailing_rows, columns = trailing.shape
    group_bits = row_bits[:2]
    group = 1 << len(group_bits)
    part = columns // group
    total_rows = trailing_rows * lax.axis_size("row")
    norm_scale = 1.0 / math.sqrt(total_rows)

    far, offsets = [panel_block], [0]
    for bit in far_bits:
        far = far + [swap(piece, "col", bit) for piece in far]
        offsets = offsets + [o ^ bit for o in offsets]
    mate = swap(panel_block, "col", near)
    last = [swap(piece, "col", near) for piece in far[1:]]
    order = [0, near] + offsets[1:] + [o ^ near for o in offsets[1:]]

    square, wide = f32(width, width), f32(width, columns)
    half_square = f32(width // 2, width)
    split_shape = jax.ShapeDtypeStruct((piece_rows, 2 * width), jnp.bfloat16)
    copies = pltpu.SemaphoreType.DMA
    gram, own_split = pl.pallas_call(
        own_kernel, out_shape=(square, split_shape), in_specs=[VMEM], out_specs=(VMEM,) * 2,
        compiler_params=limit(8), name="own", cost_estimate=COST,
    )(pltpu.with_memory_space_constraint(panel_block, pltpu.HBM))
    gram, mate_split = pl.pallas_call(
        functools.partial(mate_kernel, near=near),
        out_shape=(half_square, split_shape), in_specs=[VMEM] * 2, out_specs=(VMEM,) * 2,
        scratch_shapes=[pltpu.VMEM((width, width), jnp.float32)],
        compiler_params=limit(8), name="mate", cost_estimate=COST,
    )(mate, gram)
    held = pltpu.with_memory_space_constraint(trailing, pltpu.VMEM)
    cross = pl.pallas_call(
        functools.partial(near_kernel, order=order), out_shape=wide,
        in_specs=[VMEM] * 3, out_specs=VMEM, compiler_params=limit(16), name="near",
    )(own_split, mate_split, held)
    splits = [own_split, mate_split]
    pieces = far[1:] + last
    for i, piece in enumerate(pieces[:-1]):
        split_out, cross = pl.pallas_call(
            functools.partial(far_kernel, offset=order[i + 2]),
            out_shape=(split_shape, wide), in_specs=[VMEM] * 3,
            out_specs=(VMEM,) * 2, compiler_params=limit(16), name="far",
        )(piece, held, cross)
        splits.append(split_out)
    split_out, *parts = pl.pallas_call(
        functools.partial(last_kernel, offset=order[-1]),
        out_shape=(split_shape,) + (f32(width, part),) * group,
        in_specs=[VMEM] * 3, out_specs=(VMEM,) * (1 + group),
        scratch_shapes=[pltpu.VMEM((width, columns), jnp.float32)],
        compiler_params=limit(16), name="last",
    )(pieces[-1], held, cross)
    splits.append(split_out)

    found = [gram]
    for k in range(1, group):
        found.append(swap(gram, "row", k))
    gram = sum(found[1:], found[0])
    for bit in row_bits[len(group_bits) :]:
        gram = gram + swap(gram, "row", bit)
    halves = [gram if o == 0 else swap(gram, "col", o) for f in offsets for o in (f, f ^ near)]
    r_scaled, solve = pl.pallas_call(
        functools.partial(factor_kernel, near=near, block=BLOCK, step=STEP, norm_scale=norm_scale),
        out_shape=(square, jax.ShapeDtypeStruct((2 * width, 2 * width), jnp.bfloat16)),
        in_specs=[VMEM] * len(halves), out_specs=(VMEM, VMEM), compiler_params=limit(4), name="factor",
    )(*halves)
    for k in range(1, group):
        parts[k] = swap(parts[k], "row", k)
    mine = sum(parts[1:], parts[0])
    for bit in row_bits[len(group_bits) :]:
        mine = mine + swap(mine, "row", bit)
    others = []
    for k in range(1, group):
        others.append(swap(mine, "row", k))
    w_scaled, remainder = pl.pallas_call(
        functools.partial(final_kernel, order=order, group=group, norm_scale=norm_scale, chunk=CHUNK),
        out_shape=(wide, f32(trailing_rows, columns)),
        in_specs=[VMEM] * (2 + len(order) + group), out_specs=(HBM, HBM),
        scratch_shapes=[
            pltpu.VMEM((width, columns), jnp.float32),
            pltpu.VMEM((width, columns), jnp.float32),
            pltpu.VMEM((len(order), piece_rows, columns), jnp.float32),
            copies,
            copies((len(order), CUTS)),
        ],
        compiler_params=limit(20), name="final",
    )(solve, held, *splits, mine, *others)
    return r_scaled, w_scaled, remainder


def solution(mesh):
    in_specs = (P(("row", "col"), None), P("row", "col"))
    out_specs = (P(), P(None, "col"), P("row", "col"))

    return jax.shard_map(body, mesh=mesh, in_specs=in_specs, out_specs=out_specs, check_vma=False)
```

```python
import functools
import math

import jax
import jax.numpy as jnp
from jax import lax
from jax.experimental import pallas as pl
from jax.experimental.pallas import tpu as pltpu
from jax.sharding import PartitionSpec as P


HIGHEST = lax.Precision.HIGHEST
CUTS = 2
BLOCK, STEP = 32, 16
COST = pl.CostEstimate(flops=1 << 31, bytes_accessed=1 << 23, transcendentals=0)
CHUNK = 128
VMEM = pl.BlockSpec(memory_space=pltpu.VMEM)
HBM = pl.BlockSpec(memory_space=pltpu.HBM)


def limit(mebibytes):
    return pltpu.CompilerParams(vmem_limit_bytes=mebibytes << 20)


def f32(*shape):
    return jax.ShapeDtypeStruct(shape, jnp.float32)


def split(value):
    high = value.astype(jnp.bfloat16)
    return high, (value - high.astype(jnp.float32)).astype(jnp.bfloat16)


def store_split(split_ref, piece):
    width = piece.shape[1]
    split_ref[:, :width], split_ref[:, width:] = split(piece)


def cross_of(split_ref, block):
    width = split_ref.shape[1] // 2
    high, low = split_ref[:, :width], split_ref[:, width:]
    block_high, block_low = split(block)
    contract = ((0,), (0,))
    product = dot(high, block_high, contract)
    return product + dot(high, block_low, contract) + dot(low, block_high, contract)


def dot(first, second, dims, precision=None):
    return lax.dot_general(
        first, second, (dims, ((), ())), precision=precision, preferred_element_type=jnp.float32
    )


def block_of(offset, rows):
    return (lax.axis_index("col") ^ offset) * rows


def part_of(slot, group):
    return (lax.axis_index("row") & (group - 1)) ^ slot


def wait_all(copies):
    for copy in copies:
        copy.wait()


def own_kernel(panel_ref, gram_ref, split_ref):
    panel = panel_ref[...]
    gram_ref[...] = dot(panel, panel, ((0,), (0,)), HIGHEST)
    store_split(split_ref, panel)


def mate_kernel(mate_ref, gram_in_ref, gram_ref, split_ref, sum_ref, *, near):
    mate = mate_ref[...]
    half = mate.shape[1] // 2
    sum_ref[...] = gram_in_ref[...] + dot(mate, mate, ((0,), (0,)), HIGHEST)
    upper = jnp.where((lax.axis_index("col") & near) == 0, 0, half)
    gram_ref[...] = sum_ref[pl.ds(pl.multiple_of(upper, half), half), :]
    store_split(split_ref, mate)


def rows_of(held_ref, offset, rows):
    return held_ref[pl.ds(pl.multiple_of(block_of(offset, rows), rows), rows), :]


def near_kernel(own_ref, mate_ref, held_ref, cross_ref, *, order):
    rows = own_ref.shape[0]
    total = cross_of(own_ref, rows_of(held_ref, order[0], rows))
    cross_ref[...] = total + cross_of(mate_ref, rows_of(held_ref, order[1], rows))


def far_kernel(piece_ref, held_ref, cross_in_ref, split_ref, cross_ref, *, offset):
    store_split(split_ref, piece_ref[...])
    block = rows_of(held_ref, offset, piece_ref.shape[0])
    cross_ref[...] = cross_in_ref[...] + cross_of(split_ref, block)


def last_kernel(piece_ref, held_ref, cross_in_ref, split_ref, *refs, offset):
    *part_refs, sum_ref = refs
    store_split(split_ref, piece_ref[...])
    block = rows_of(held_ref, offset, piece_ref.shape[0])
    sum_ref[...] = cross_in_ref[...] + cross_of(split_ref, block)
    part = part_refs[0].shape[1]
    for k, part_ref in enumerate(part_refs):
        first = pl.multiple_of(part_of(k, len(part_refs)) * part, part)
        part_ref[...] = sum_ref[:, pl.ds(first, part)]


def factor_kernel(*refs, near, block, step, norm_scale):
    *half_refs, scaled_ref, solve_ref = refs
    width = scaled_ref.shape[1]
    first_half = (lax.axis_index("col") & near) == 0
    mine, other = (sum(ref[...] for ref in half_refs[k::2]) for k in range(2))
    gram = jnp.concatenate(
        [jnp.where(first_half, mine, other), jnp.where(first_half, other, mine)], 0
    )
    local = lax.broadcasted_iota(jnp.int32, (step, 1), 0)
    lanes = lax.broadcasted_iota(jnp.int32, (block, width), 1)
    rows = lax.broadcasted_iota(jnp.int32, (block, width), 0)
    factor_rows, inverse_rows = [], []
    for first in range(0, width, block):
        left = gram[first : first + block, :]
        right = jnp.where(lanes == rows + first, 1.0, 0.0)
        if factor_rows:
            above = jnp.concatenate(factor_rows, 0)
            both = jnp.concatenate([above, jnp.concatenate(inverse_rows, 0)], 1)
            update = dot(above[:, first : first + block], both, ((0,), (0,)), HIGHEST)
            left = left - update[:, :width]
            right = right - update[:, width:]
        left_done, right_done = [], []
        for start in range(first, first + block, step):
            columns = [
                jnp.broadcast_to(left[:, start + j : start + j + 1], left.shape) for j in range(step)
            ]
            pivots = jnp.ones((step, width), jnp.float32)
            for k in range(step):
                pivot = columns[k][k : k + 1, :]
                pivots = jnp.where(local == k, pivot, pivots)
                ratio = columns[k] * (1.0 / pivot)
                for j in range(k + 1, step):
                    columns[j] = columns[j] - ratio * columns[j][k : k + 1, :]
                head = jnp.where(local > k, ratio[:step], 0.0)
                if ratio.shape[0] > step:
                    head = jnp.concatenate([head, ratio[step:]], 0)
                columns[k] = head
            for k in range(step):
                left = left - columns[k] * left[k : k + 1, :]
                right = right - columns[k] * right[k : k + 1, :]
            scale = lax.rsqrt(pivots)
            left_done.append(left[:step] * scale)
            right_done.append(right[:step] * scale)
            left, right = left[step:], right[step:]
        factor_rows.append(jnp.where(lanes >= rows + first, jnp.concatenate(left_done, 0), 0.0))
        inverse_rows.append(jnp.where(lanes <= rows + first, jnp.concatenate(right_done, 0), 0.0))
        scaled_ref[first : first + block, :] = factor_rows[-1] * norm_scale
    inverse = jnp.concatenate(inverse_rows, 0)
    store_split(solve_ref.at[:width], inverse)
    high, low = split(inverse)
    left, right = jnp.concatenate([high, high, low], 0), jnp.concatenate([high, low, high], 0)
    store_split(solve_ref.at[width:], dot(left, right, ((0,), (0,))))


def final_kernel(solve_ref, held_ref, *refs, order, group, norm_scale, chunk):
    split_refs, refs = refs[: len(order)], refs[len(order) :]
    part_refs, (w_ref, remainder_ref, cross_ref, w_here, result, w_sem, sems) = refs[:group], refs[group:]
    width, part = part_refs[0].shape
    for k, part_ref in enumerate(part_refs):
        where = pl.ds(pl.multiple_of(part_of(k, group) * part, part), part)
        high, low = split(part_ref[...])
        cross_ref[:width, where] = high
        cross_ref[width : 2 * width, where] = high
        cross_ref[2 * width :, where] = low
    contract = ((1,), (0,))
    before = cross_ref[...]

    def solved(part):
        both = solve_ref[part * width : (part + 1) * width, :]
        return dot(jnp.concatenate([both, both[:, :width]], 1), before, contract)

    high, low = split(solved(1))
    right = jnp.concatenate([high, high, low], 0)
    copies = []
    rows = split_refs[0].shape[0]
    cuts = sems.shape[1]
    for i, split_ref in enumerate(split_refs):
        base = pl.multiple_of(block_of(order[i], rows), rows)
        for first in range(0, rows, chunk):
            both = split_ref[first : first + chunk, :]
            product = dot(jnp.concatenate([both, both[:, :width]], 1), right, contract)
            held = held_ref[pl.ds(pl.multiple_of(base + first, chunk), chunk), :]
            result[i, first : first + chunk, :] = held - product
            done = first + chunk
            if done % (rows // cuts) == 0:
                n = done * cuts // rows - 1
                here = pl.ds(n * (rows // cuts), rows // cuts)
                there = pl.ds(pl.multiple_of(base + n * (rows // cuts), rows // cuts), rows // cuts)
                copies.append(
                    pltpu.make_async_copy(result.at[i, here], remainder_ref.at[there], sems.at[i, n])
                )
                copies[-1].start()
        if i == 0:
            w_here[...] = solved(0) * norm_scale
            copies.append(pltpu.make_async_copy(w_here, w_ref, w_sem))
            copies[-1].start()
    wait_all(copies)


def swap(value, axis, bit):
    size = lax.axis_size(axis)
    return lax.ppermute(value, axis, [(i, i ^ bit) for i in range(size)])


def bits_of(axis):
    size = lax.axis_size(axis)
    assert size & (size - 1) == 0
    return [1 << b for b in range(size.bit_length() - 1)]


def body(panel_block, trailing):
    row_bits, col_bits = bits_of("row"), bits_of("col")
    near, far_bits = col_bits[0], col_bits[1:]
    piece_rows, width = panel_block.shape
    trailing_rows, columns = trailing.shape
    group_bits = row_bits[:2]
    group = 1 << len(group_bits)
    part = columns // group
    total_rows = trailing_rows * lax.axis_size("row")
    norm_scale = 1.0 / math.sqrt(total_rows)

    far, offsets = [panel_block], [0]
    for bit in far_bits:
        far = far + [swap(piece, "col", bit) for piece in far]
        offsets = offsets + [o ^ bit for o in offsets]
    mate = swap(panel_block, "col", near)
    last = [swap(piece, "col", near) for piece in far[1:]]
    order = [0, near] + offsets[1:] + [o ^ near for o in offsets[1:]]

    square, wide = f32(width, width), f32(width, columns)
    half_square = f32(width // 2, width)
    split_shape = jax.ShapeDtypeStruct((piece_rows, 2 * width), jnp.bfloat16)
    copies = pltpu.SemaphoreType.DMA
    gram, own_split = pl.pallas_call(
        own_kernel, out_shape=(square, split_shape), in_specs=[VMEM], out_specs=(VMEM,) * 2,
        compiler_params=limit(8), name="own", cost_estimate=COST,
    )(pltpu.with_memory_space_constraint(panel_block, pltpu.HBM))
    gram, mate_split = pl.pallas_call(
        functools.partial(mate_kernel, near=near),
        out_shape=(half_square, split_shape), in_specs=[VMEM] * 2, out_specs=(VMEM,) * 2,
        scratch_shapes=[pltpu.VMEM((width, width), jnp.float32)],
        compiler_params=limit(8), name="mate", cost_estimate=COST,
    )(mate, gram)
    held = pltpu.with_memory_space_constraint(trailing, pltpu.VMEM)
    cross = pl.pallas_call(
        functools.partial(near_kernel, order=order), out_shape=wide,
        in_specs=[VMEM] * 3, out_specs=VMEM, compiler_params=limit(16), name="near",
    )(own_split, mate_split, held)
    splits = [own_split, mate_split]
    pieces = far[1:] + last
    for i, piece in enumerate(pieces[:-1]):
        split_out, cross = pl.pallas_call(
            functools.partial(far_kernel, offset=order[i + 2]),
            out_shape=(split_shape, wide), in_specs=[VMEM] * 3,
            out_specs=(VMEM,) * 2, compiler_params=limit(16), name="far",
        )(piece, held, cross)
        splits.append(split_out)
    split_out, *parts = pl.pallas_call(
        functools.partial(last_kernel, offset=order[-1]),
        out_shape=(split_shape,) + (f32(width, part),) * group,
        in_specs=[VMEM] * 3, out_specs=(VMEM,) * (1 + group),
        scratch_shapes=[pltpu.VMEM((width, columns), jnp.float32)],
        compiler_params=limit(16), name="last",
    )(pieces[-1], held, cross)
    splits.append(split_out)

    found = [gram]
    for k in range(1, group):
        found.append(swap(gram, "row", k))
    gram = sum(found[1:], found[0])
    for bit in row_bits[len(group_bits) :]:
        gram = gram + swap(gram, "row", bit)
    halves = [gram if o == 0 else swap(gram, "col", o) for f in offsets for o in (f, f ^ near)]
    r_scaled, solve = pl.pallas_call(
        functools.partial(factor_kernel, near=near, block=BLOCK, step=STEP, norm_scale=norm_scale),
        out_shape=(square, jax.ShapeDtypeStruct((2 * width, 2 * width), jnp.bfloat16)),
        in_specs=[VMEM] * len(halves), out_specs=(VMEM, VMEM), compiler_params=limit(4), name="factor",
    )(*halves)
    for k in range(1, group):
        parts[k] = swap(parts[k], "row", k)
    mine = sum(parts[1:], parts[0])
    for bit in row_bits[len(group_bits) :]:
        mine = mine + swap(mine, "row", bit)
    others = []
    for k in range(1, group):
        others.append(swap(mine, "row", k))
    w_scaled, remainder = pl.pallas_call(
        functools.partial(final_kernel, order=order, group=group, norm_scale=norm_scale, chunk=CHUNK),
        out_shape=(wide, f32(trailing_rows, columns)),
        in_specs=[VMEM] * (2 + len(order) + group), out_specs=(HBM, HBM),
        scratch_shapes=[
            pltpu.VMEM((3 * width, columns), jnp.bfloat16),
            pltpu.VMEM((width, columns), jnp.float32),
            pltpu.VMEM((len(order), piece_rows, columns), jnp.float32),
            copies,
            copies((len(order), CUTS)),
        ],
        compiler_params=limit(20), name="final",
    )(solve, held, *splits, mine, *others)
    return r_scaled, w_scaled, remainder


def solution(mesh):
    in_specs = (P(("row", "col"), None), P("row", "col"))
    out_specs = (P(), P(None, "col"), P("row", "col"))

    return jax.shard_map(body, mesh=mesh, in_specs=in_specs, out_specs=out_specs, check_vma=False)
```

```python
import functools
import math

import jax
import jax.numpy as jnp
from jax import lax
from jax.experimental import pallas as pl
from jax.experimental.pallas import tpu as pltpu
from jax.sharding import PartitionSpec as P


HIGHEST = lax.Precision.HIGHEST
CUTS = 4
BLOCK, STEP = 32, 16
COST = pl.CostEstimate(flops=1 << 31, bytes_accessed=1 << 23, transcendentals=0)
CHUNK = 128
VMEM = pl.BlockSpec(memory_space=pltpu.VMEM)
HBM = pl.BlockSpec(memory_space=pltpu.HBM)


def limit(mebibytes):
    return pltpu.CompilerParams(vmem_limit_bytes=mebibytes << 20)


def f32(*shape):
    return jax.ShapeDtypeStruct(shape, jnp.float32)


def split(value):
    high = value.astype(jnp.bfloat16)
    return high, (value - high.astype(jnp.float32)).astype(jnp.bfloat16)


def store_split(split_ref, piece):
    width = piece.shape[1]
    split_ref[:, :width], split_ref[:, width:] = split(piece)


def cross_of(split_ref, block):
    width = split_ref.shape[1] // 2
    high, low = split_ref[:, :width], split_ref[:, width:]
    block_high, block_low = split(block)
    contract = ((0,), (0,))
    product = dot(high, block_high, contract)
    return product + dot(high, block_low, contract) + dot(low, block_high, contract)


def dot(first, second, dims, precision=None):
    return lax.dot_general(
        first, second, (dims, ((), ())), precision=precision, preferred_element_type=jnp.float32
    )


def block_of(offset, rows):
    return (lax.axis_index("col") ^ offset) * rows


def part_of(slot, group):
    return (lax.axis_index("row") & (group - 1)) ^ slot


def wait_all(copies):
    for copy in copies:
        copy.wait()


def own_kernel(panel_ref, gram_ref, split_ref):
    panel = panel_ref[...]
    gram_ref[...] = dot(panel, panel, ((0,), (0,)), HIGHEST)
    store_split(split_ref, panel)


def mate_kernel(mate_ref, gram_in_ref, gram_ref, split_ref, sum_ref, *, near):
    mate = mate_ref[...]
    half = mate.shape[1] // 2
    sum_ref[...] = gram_in_ref[...] + dot(mate, mate, ((0,), (0,)), HIGHEST)
    upper = jnp.where((lax.axis_index("col") & near) == 0, 0, half)
    gram_ref[...] = sum_ref[pl.ds(pl.multiple_of(upper, half), half), :]
    store_split(split_ref, mate)


def rows_of(held_ref, offset, rows):
    return held_ref[pl.ds(pl.multiple_of(block_of(offset, rows), rows), rows), :]


def near_kernel(own_ref, mate_ref, held_ref, cross_ref, *, order):
    rows = own_ref.shape[0]
    total = cross_of(own_ref, rows_of(held_ref, order[0], rows))
    cross_ref[...] = total + cross_of(mate_ref, rows_of(held_ref, order[1], rows))


def far_kernel(piece_ref, held_ref, cross_in_ref, split_ref, cross_ref, *, offset):
    store_split(split_ref, piece_ref[...])
    block = rows_of(held_ref, offset, piece_ref.shape[0])
    cross_ref[...] = cross_in_ref[...] + cross_of(split_ref, block)


def last_kernel(piece_ref, held_ref, cross_in_ref, split_ref, *refs, offset):
    *part_refs, sum_ref = refs
    store_split(split_ref, piece_ref[...])
    block = rows_of(held_ref, offset, piece_ref.shape[0])
    sum_ref[...] = cross_in_ref[...] + cross_of(split_ref, block)
    part = part_refs[0].shape[1]
    for k, part_ref in enumerate(part_refs):
        first = pl.multiple_of(part_of(k, len(part_refs)) * part, part)
        part_ref[...] = sum_ref[:, pl.ds(first, part)]


def factor_kernel(*refs, near, block, step, norm_scale):
    *half_refs, scaled_ref, solve_ref = refs
    width = scaled_ref.shape[1]
    first_half = (lax.axis_index("col") & near) == 0
    mine, other = (sum(ref[...] for ref in half_refs[k::2]) for k in range(2))
    gram = jnp.concatenate(
        [jnp.where(first_half, mine, other), jnp.where(first_half, other, mine)], 0
    )
    local = lax.broadcasted_iota(jnp.int32, (step, 1), 0)
    lanes = lax.broadcasted_iota(jnp.int32, (block, width), 1)
    rows = lax.broadcasted_iota(jnp.int32, (block, width), 0)
    factor_rows, inverse_rows = [], []
    for first in range(0, width, block):
        left = gram[first : first + block, :]
        right = jnp.where(lanes == rows + first, 1.0, 0.0)
        if factor_rows:
            above = jnp.concatenate(factor_rows, 0)
            both = jnp.concatenate([above, jnp.concatenate(inverse_rows, 0)], 1)
            update = dot(above[:, first : first + block], both, ((0,), (0,)), HIGHEST)
            left = left - update[:, :width]
            right = right - update[:, width:]
        left_done, right_done = [], []
        for start in range(first, first + block, step):
            columns = [
                jnp.broadcast_to(left[:, start + j : start + j + 1], left.shape) for j in range(step)
            ]
            pivots = jnp.ones((step, width), jnp.float32)
            for k in range(step):
                pivot = columns[k][k : k + 1, :]
                pivots = jnp.where(local == k, pivot, pivots)
                ratio = columns[k] * (1.0 / pivot)
                for j in range(k + 1, step):
                    columns[j] = columns[j] - ratio * columns[j][k : k + 1, :]
                head = jnp.where(local > k, ratio[:step], 0.0)
                if ratio.shape[0] > step:
                    head = jnp.concatenate([head, ratio[step:]], 0)
                columns[k] = head
            for k in range(step):
                left = left - columns[k] * left[k : k + 1, :]
                right = right - columns[k] * right[k : k + 1, :]
            scale = lax.rsqrt(pivots)
            left_done.append(left[:step] * scale)
            right_done.append(right[:step] * scale)
            left, right = left[step:], right[step:]
        factor_rows.append(jnp.where(lanes >= rows + first, jnp.concatenate(left_done, 0), 0.0))
        inverse_rows.append(jnp.where(lanes <= rows + first, jnp.concatenate(right_done, 0), 0.0))
        scaled_ref[first : first + block, :] = factor_rows[-1] * norm_scale
    inverse = jnp.concatenate(inverse_rows, 0)
    store_split(solve_ref.at[:width], inverse)
    high, low = split(inverse)
    left, right = jnp.concatenate([high, high, low], 0), jnp.concatenate([high, low, high], 0)
    store_split(solve_ref.at[width:], dot(left, right, ((0,), (0,))))


def final_kernel(solve_ref, held_ref, *refs, order, group, norm_scale, chunk):
    split_refs, refs = refs[: len(order)], refs[len(order) :]
    part_refs, (w_ref, remainder_ref, cross_ref, w_here, result, w_sem, sems) = refs[:group], refs[group:]
    width, part = part_refs[0].shape
    for k, part_ref in enumerate(part_refs):
        cross_ref[:, pl.ds(pl.multiple_of(part_of(k, group) * part, part), part)] = part_ref[...]
    contract = ((1,), (0,))
    high, low = split(cross_ref[...])
    before = jnp.concatenate([high, high, low], 0)

    def solved(part):
        both = solve_ref[part * width : (part + 1) * width, :]
        return dot(jnp.concatenate([both, both[:, :width]], 1), before, contract)

    high, low = split(solved(1))
    right = jnp.concatenate([high, high, low], 0)
    copies = []
    rows = split_refs[0].shape[0]
    cuts = sems.shape[1]
    for i, split_ref in enumerate(split_refs):
        base = pl.multiple_of(block_of(order[i], rows), rows)
        for first in range(0, rows, chunk):
            both = split_ref[first : first + chunk, :]
            product = dot(jnp.concatenate([both, both[:, :width]], 1), right, contract)
            held = held_ref[pl.ds(pl.multiple_of(base + first, chunk), chunk), :]
            result[i, first : first + chunk, :] = held - product
            done = first + chunk
            if done % (rows // cuts) == 0:
                n = done * cuts // rows - 1
                here = pl.ds(n * (rows // cuts), rows // cuts)
                there = pl.ds(pl.multiple_of(base + n * (rows // cuts), rows // cuts), rows // cuts)
                copies.append(
                    pltpu.make_async_copy(result.at[i, here], remainder_ref.at[there], sems.at[i, n])
                )
                copies[-1].start()
        if i == 0:
            w_here[...] = solved(0) * norm_scale
            copies.append(pltpu.make_async_copy(w_here, w_ref, w_sem))
            copies[-1].start()
    wait_all(copies)


def swap(value, axis, bit):
    size = lax.axis_size(axis)
    return lax.ppermute(value, axis, [(i, i ^ bit) for i in range(size)])


def bits_of(axis):
    size = lax.axis_size(axis)
    assert size & (size - 1) == 0
    return [1 << b for b in range(size.bit_length() - 1)]


def body(panel_block, trailing):
    row_bits, col_bits = bits_of("row"), bits_of("col")
    near, far_bits = col_bits[0], col_bits[1:]
    piece_rows, width = panel_block.shape
    trailing_rows, columns = trailing.shape
    group_bits = row_bits[:2]
    group = 1 << len(group_bits)
    part = columns // group
    total_rows = trailing_rows * lax.axis_size("row")
    norm_scale = 1.0 / math.sqrt(total_rows)

    far, offsets = [panel_block], [0]
    for bit in far_bits:
        far = far + [swap(piece, "col", bit) for piece in far]
        offsets = offsets + [o ^ bit for o in offsets]
    mate = swap(panel_block, "col", near)
    last = [swap(piece, "col", near) for piece in far[1:]]
    order = [0, near] + offsets[1:] + [o ^ near for o in offsets[1:]]

    square, wide = f32(width, width), f32(width, columns)
    half_square = f32(width // 2, width)
    split_shape = jax.ShapeDtypeStruct((piece_rows, 2 * width), jnp.bfloat16)
    copies = pltpu.SemaphoreType.DMA
    gram, own_split = pl.pallas_call(
        own_kernel, out_shape=(square, split_shape), in_specs=[VMEM], out_specs=(VMEM,) * 2,
        compiler_params=limit(8), name="own", cost_estimate=COST,
    )(pltpu.with_memory_space_constraint(panel_block, pltpu.HBM))
    gram, mate_split = pl.pallas_call(
        functools.partial(mate_kernel, near=near),
        out_shape=(half_square, split_shape), in_specs=[VMEM] * 2, out_specs=(VMEM,) * 2,
        scratch_shapes=[pltpu.VMEM((width, width), jnp.float32)],
        compiler_params=limit(8), name="mate", cost_estimate=COST,
    )(mate, gram)
    held = pltpu.with_memory_space_constraint(trailing, pltpu.VMEM)
    cross = pl.pallas_call(
        functools.partial(near_kernel, order=order), out_shape=wide,
        in_specs=[VMEM] * 3, out_specs=VMEM, compiler_params=limit(16), name="near",
    )(own_split, mate_split, held)
    splits = [own_split, mate_split]
    pieces = far[1:] + last
    for i, piece in enumerate(pieces[:-1]):
        split_out, cross = pl.pallas_call(
            functools.partial(far_kernel, offset=order[i + 2]),
            out_shape=(split_shape, wide), in_specs=[VMEM] * 3,
            out_specs=(VMEM,) * 2, compiler_params=limit(16), name="far",
        )(piece, held, cross)
        splits.append(split_out)
    split_out, *parts = pl.pallas_call(
        functools.partial(last_kernel, offset=order[-1]),
        out_shape=(split_shape,) + (f32(width, part),) * group,
        in_specs=[VMEM] * 3, out_specs=(VMEM,) * (1 + group),
        scratch_shapes=[pltpu.VMEM((width, columns), jnp.float32)],
        compiler_params=limit(16), name="last",
    )(pieces[-1], held, cross)
    splits.append(split_out)

    found = [gram]
    for k in range(1, group):
        found.append(swap(gram, "row", k))
    gram = sum(found[1:], found[0])
    for bit in row_bits[len(group_bits) :]:
        gram = gram + swap(gram, "row", bit)
    halves = [gram if o == 0 else swap(gram, "col", o) for f in offsets for o in (f, f ^ near)]
    r_scaled, solve = pl.pallas_call(
        functools.partial(factor_kernel, near=near, block=BLOCK, step=STEP, norm_scale=norm_scale),
        out_shape=(square, jax.ShapeDtypeStruct((2 * width, 2 * width), jnp.bfloat16)),
        in_specs=[VMEM] * len(halves), out_specs=(VMEM, VMEM), compiler_params=limit(4), name="factor",
    )(*halves)
    for k in range(1, group):
        parts[k] = swap(parts[k], "row", k)
    mine = sum(parts[1:], parts[0])
    for bit in row_bits[len(group_bits) :]:
        mine = mine + swap(mine, "row", bit)
    others = []
    for k in range(1, group):
        others.append(swap(mine, "row", k))
    w_scaled, remainder = pl.pallas_call(
        functools.partial(final_kernel, order=order, group=group, norm_scale=norm_scale, chunk=CHUNK),
        out_shape=(wide, f32(trailing_rows, columns)),
        in_specs=[VMEM] * (2 + len(order) + group), out_specs=(HBM, HBM),
        scratch_shapes=[
            pltpu.VMEM((width, columns), jnp.float32),
            pltpu.VMEM((width, columns), jnp.float32),
            pltpu.VMEM((len(order), piece_rows, columns), jnp.float32),
            copies,
            copies((len(order), CUTS)),
        ],
        compiler_params=limit(20), name="final",
    )(solve, held, *splits, mine, *others)
    return r_scaled, w_scaled, remainder


def solution(mesh):
    in_specs = (P(("row", "col"), None), P("row", "col"))
    out_specs = (P(), P(None, "col"), P("row", "col"))

    return jax.shard_map(body, mesh=mesh, in_specs=in_specs, out_specs=out_specs, check_vma=False)
```
